32 devices in a mesh: fsdp: 8 (over z, x), tensor: 2 (over y), dp: 2 (over core).
Axes of the slice: x: 2, y: 2, z: 4, core: 2. Of those that a mesh axis runs over, the one named last changes fastest.
Arguments:
- states: bfloat16 [4096, 4096], P('fsdp', ('tensor', 'dp')), may hold values from -6 to 6
- fresh_rows: bfloat16 [4096, 4096], P('fsdp', ('tensor', 'dp')), may hold values from -6 to 6
- norm_gain: bfloat16 [4096], P(('tensor', 'dp')), may hold values from 0.25 to 1.75
- gate_weight: bfloat16 [4096, 8192], P('fsdp', ('tensor', 'dp')), may hold values from -0.09375 to 0.09375
- up_weight: bfloat16 [4096, 8192], P('fsdp', ('tensor', 'dp')), may hold values from -0.09375 to 0.09375
- down_weight: bfloat16 [8192, 4096], P(('tensor', 'dp'), 'fsdp'), may hold values from -0.09375 to 0.09375
- halted: int32 [64, 64], P('fsdp'), may hold values from 0 to 1, as said below
- refill_index: int32 [64, 64], P('fsdp'), may hold values from 0 to 63, each once within a row
Outputs:
- next_states: bfloat16 [4096, 4096], P('fsdp', ('tensor', 'dp'))
The draws below stay inside these ranges and needn't reach their ends.
Inputs may be any that keep to these rules, and one draw needn't show every extreme that they name: In each aligned block of 512 rows (in row order over all batches) at most 384 rows are running (halted 0), and some block has exactly 384 running rows. Each batch's row of refill_index holds every number of 0 to 63 once.
All inputs are finite; a program needn't handle non-finite values.
Results may differ from the reference program's by a relative error of at most 0.0085.
Values may be sent and summed in bfloat16 or wider, within the bound.
A program may use at most 128 MiB of HBM per device.

```python
import jax
import jax.numpy as jnp
from jax import lax

D = 4096
FF = 8192
BATCH = 64
ROWS_DEV = 512
ACT_MAX = 384
TOKENS = 4096
NBATCH = 64
N_TENSOR = 2
N_DP = 2


def draw_halted(key, part):
    block_count = TOKENS // ROWS_DEV
    key_count = jax.random.fold_in(key, 11)
    key_top = jax.random.fold_in(key, 12)
    key_rank = jax.random.fold_in(key, 13)
    counts = jax.random.randint(key_count, (block_count,), 1, ACT_MAX + 1)
    chosen = jax.random.randint(key_top, (), 0, block_count)
    counts = jnp.where(jnp.arange(block_count) == chosen, ACT_MAX, counts)
    block_keys = jax.random.split(key_rank, block_count)
    rank_table = jax.vmap(lambda single_key: jax.random.permutation(single_key, ROWS_DEV))(block_keys)
    running = rank_table < counts[:, None]
    stopped = 1 - running.astype(jnp.int32)
    return stopped.reshape(TOKENS // BATCH, BATCH).astype(jnp.int32)


def raised(result, own_key, source, target, shards_of, factor):
    def block_of(position):
        return (jnp.arange(result.shape[position]) // (result.shape[position] // shards_of)).reshape((-1,) + (1,) * (result.ndim - 1 - position))

    one_side = jax.random.permutation(own_key, shards_of)[block_of(target)]
    second = (block_of(target) + shards_of // 2) % shards_of
    return jnp.where((block_of(source) == one_side) | (block_of(source) == second), factor * result, result)


def levels(rng, shape, cuts, least, largest):
    level, own = 1.0, jax.random.fold_in(rng, 6)
    for position, parts in cuts:
        draws = jnp.exp(jax.random.uniform(jax.random.fold_in(own, position), (parts,), jnp.float32, least / len(cuts), largest / len(cuts)))
        level = level * jnp.repeat(draws, shape[position] // parts).reshape([-1 if axis == position else 1 for axis in range(len(shape))])
    return level


def noise(own_key, extent, spread, bound, pieces=(), dtype=jnp.bfloat16):
    gain = levels(own_key, extent, pieces, -0.22, 0.18) if pieces else 1.0
    result = jax.random.normal(own_key, extent, jnp.float32) * spread * gain
    return jnp.minimum(jnp.maximum(result, -bound), bound).astype(dtype)


def heavy_noise(rng, shape, scale, most, pieces, heavy, kind=jnp.bfloat16):
    array = scale * jax.random.normal(rng, shape, jnp.float32)
    if pieces:
        array = array * levels(rng, shape, pieces, -0.22, 0.18)
    return jnp.clip(raised(array, jax.random.fold_in(rng, 3), *heavy), -most, most).astype(kind)


def setup_inputs(seed: int = 0) -> dict:
    keys = jax.random.split(jax.random.key(seed), 9)
    states = noise(keys[0], (TOKENS, D), 1.0, 6.0, ((0, 8), (1, 4)))
    fresh_rows = noise(keys[1], (TOKENS, D), 1.0, 6.0, ((0, 8), (1, 4)))
    norm_gain = jnp.clip(1.0 + 0.15 * jax.random.normal(keys[2], (D,), jnp.float32), 0.25, 1.75).astype(jnp.bfloat16)
    gate_weight = noise(keys[3], (D, FF), D ** -0.5, 0.09375, ((0, 8), (1, 4)))
    up_weight = noise(keys[4], (D, FF), D ** -0.5, 0.09375, ((0, 8), (1, 4)))
    down_weight = heavy_noise(keys[5], (FF, D), FF ** -0.5, 0.09375, ((0, 4), (1, 8)), (0, 1, 8, 2.0))
    halted = draw_halted(jax.random.fold_in(keys[8], 71), 0)
    refill_index = jax.vmap(lambda own: jax.random.permutation(own, BATCH))(jax.random.split(keys[7], NBATCH)).reshape((NBATCH, BATCH)).astype(jnp.int32)
    return {"states": states, "fresh_rows": fresh_rows, "norm_gain": norm_gain, "gate_weight": gate_weight, "up_weight": up_weight, "down_weight": down_weight, "halted": halted, "refill_index": refill_index}


norm_eps = 1e-05

def reference(states, fresh_rows, norm_gain, gate_weight, up_weight, down_weight, halted, refill_index):
    widened = states.astype(jnp.float32)
    mean_square = lax.optimization_barrier(jnp.mean(widened * widened, axis=-1, keepdims=True))
    normed = (widened * lax.rsqrt(mean_square + norm_eps) * norm_gain.astype(jnp.float32)).astype(jnp.bfloat16)
    gate_sum = jnp.dot(normed, gate_weight, preferred_element_type=jnp.float32)
    up_sum = jnp.dot(normed, up_weight, preferred_element_type=jnp.float32)
    hidden = (jax.nn.silu(gate_sum) * up_sum).astype(jnp.bfloat16)
    groups = N_TENSOR * N_DP
    group_width = FF // groups
    hidden_groups = hidden.reshape(TOKENS, groups, group_width).transpose(1, 0, 2)
    down_groups = down_weight.reshape(groups, group_width, D)

    def accumulate(running_sum, group_pair):
        hidden_part, weight_part = group_pair
        partial_value = jnp.dot(hidden_part, weight_part, preferred_element_type=jnp.float32)
        rounded = lax.optimization_barrier(partial_value.astype(jnp.bfloat16))
        return (running_sum + rounded.astype(jnp.float32), None)
    update, _ = lax.scan(accumulate, jnp.zeros((TOKENS, D), jnp.float32), (hidden_groups, down_groups))
    fresh_blocks = fresh_rows.reshape(NBATCH, BATCH, D)
    refilled = jax.vmap(lambda block_rows, pick_index: block_rows[pick_index])(fresh_blocks, refill_index)
    refilled = refilled.reshape(TOKENS, D)
    stopped = (halted.reshape(TOKENS) == 1)[:, None]
    computed = (widened + update).astype(jnp.bfloat16)
    return jnp.where(stopped, refilled, computed)
```

```python
import jax
import jax.numpy as jnp
from jax import lax
from jax.sharding import PartitionSpec as P

norm_eps = 1e-05


def make_body(mesh):
    count_f = mesh.shape["fsdp"]
    count_t = mesh.shape["tensor"]
    count_c = mesh.shape["dp"]
    ring = min(4, max(1, count_f // 2))
    span = count_f // ring

    def send_f(value, step_a, step_b):
        pairs = []
        for a in range(ring):
            for b in range(span):
                pairs.append((a * span + b, ((a + step_a) % ring) * span + (b + step_b) % span))
        return lax.ppermute(value, "fsdp", pairs)

    def send_axis(value, axis, count, step):
        return lax.ppermute(value, axis, [(i, (i + step) % count) for i in range(count)])

    def move_weight(weight, split_axis):
        f = lax.axis_index("fsdp")
        a, b = f // span, f % span
        join_axis = 1 - split_axis
        part = weight.shape[split_axis] // ring
        width = weight.shape[join_axis]
        pieces = [(lax.dynamic_slice_in_dim(weight, a * part, part, split_axis), f)]
        for step in range(1, ring):
            target = (a + step) % ring
            piece = lax.dynamic_slice_in_dim(weight, target * part, part, split_axis)
            pieces.append((send_f(piece, step, 0), ((a - step) % ring) * span + b))
        for piece, owner in list(pieces):
            for step in range(1, span):
                other = (owner // span) * span + (b - step) % span
                pieces.append((send_f(piece, 0, step), other))
        shape = [part, part]
        shape[join_axis] = width * count_f
        whole = jnp.zeros(shape, weight.dtype)
        for piece, owner in pieces:
            whole = lax.dynamic_update_slice_in_dim(whole, piece, owner * width, join_axis)
        return whole

    def block_update(source, norm_gain, gate_weight, up_weight, down_weight):
        a = lax.axis_index("fsdp") // span
        t = lax.axis_index("tensor")
        c = lax.axis_index("dp")
        capacity, width = source.shape
        features = width * count_t * count_c
        widened = source.astype(jnp.float32)
        mean_square = (
            lax.psum(jnp.sum(widened * widened, axis=-1, keepdims=True), ("tensor", "dp")) / features
        )
        normed = (
            widened * lax.rsqrt(mean_square + norm_eps) * norm_gain.astype(jnp.float32)
        ).astype(jnp.bfloat16)
        gate_full = move_weight(gate_weight, 1)
        up_full = move_weight(up_weight, 1)
        rows = jnp.concatenate([normed] + [send_f(normed, step, 0) for step in range(1, ring)], axis=0)
        by_tensor = [(rows, t)]
        for step in range(1, count_t):
            by_tensor.append((send_axis(rows, "tensor", count_t, step), (t - step) % count_t))
        blocks = [(piece, owner, c) for piece, owner in by_tensor]
        for step in range(1, count_c):
            for piece, owner in by_tensor:
                blocks.append((send_axis(piece, "dp", count_c, step), owner, (c - step) % count_c))
        full = jnp.zeros((capacity * ring, features), jnp.bfloat16)
        for piece, owner_t, owner_c in blocks:
            full = lax.dynamic_update_slice_in_dim(
                full, piece, (owner_t * count_c + owner_c) * width, 1
            )
        gate_sum = jnp.dot(full, gate_full, preferred_element_type=jnp.float32)
        up_sum = jnp.dot(full, up_full, preferred_element_type=jnp.float32)
        hidden = (jax.nn.silu(gate_sum) * up_sum).astype(jnp.bfloat16)
        down_full = move_weight(down_weight, 0)
        total = None
        for slot in list(range(1, ring)) + [0]:
            part = lax.slice_in_dim(hidden, slot * capacity, (slot + 1) * capacity, axis=0)
            product = jnp.dot(part, down_full, preferred_element_type=jnp.float32).astype(jnp.bfloat16)
            product = product.reshape(capacity, count_t, count_c, width)
            own = lax.dynamic_index_in_dim(product, c, 2, keepdims=False).astype(jnp.float32)
            for step in range(1, count_c):
                away = lax.dynamic_index_in_dim(product, (c + step) % count_c, 2, keepdims=False)
                own = own + send_axis(away, "dp", count_c, step).astype(jnp.float32)
            own = own.astype(jnp.bfloat16)
            mine = lax.dynamic_index_in_dim(own, t, 1, keepdims=False).astype(jnp.float32)
            for step in range(1, count_t):
                away = lax.dynamic_index_in_dim(own, (t + step) % count_t, 1, keepdims=False)
                mine = mine + send_axis(away, "tensor", count_t, step).astype(jnp.float32)
            if slot:
                mine = send_f(mine.astype(jnp.bfloat16), -slot, 0).astype(jnp.float32)
            total = mine if total is None else total + mine
        return total

    def body(states, fresh_rows, norm_gain, gate_weight, up_weight, down_weight, halted, refill_index):
        row_count = states.shape[0]
        running = halted.reshape(row_count) == 0
        capacity = row_count * 3 // 4
        slot_of = jnp.cumsum(running.astype(jnp.int32)) - 1
        slot_ids = lax.iota(jnp.int32, capacity)
        picker = ((slot_of[None, :] == slot_ids[:, None]) & running[None, :]).astype(jnp.bfloat16)
        source = jnp.dot(picker, states, preferred_element_type=jnp.float32).astype(jnp.bfloat16)
        compact = block_update(source, norm_gain, gate_weight, up_weight, down_weight)
        update = jnp.take(compact, jnp.clip(slot_of, 0, capacity - 1), axis=0)
        block_total = refill_index.shape[0]
        batch_len = refill_index.shape[1]
        fresh_blocks = fresh_rows.reshape(block_total, batch_len, fresh_rows.shape[1])
        refilled = jax.vmap(lambda block_rows, pick_index: block_rows[pick_index])(
            fresh_blocks, refill_index
        )
        refilled = refilled.reshape(row_count, fresh_rows.shape[1])
        computed = (states.astype(jnp.float32) + update).astype(jnp.bfloat16)
        return jnp.where(running[:, None], computed, refilled)

    return body


def solution(mesh):
    in_specs = (
        P("fsdp", ("tensor", "dp")),
        P("fsdp", ("tensor", "dp")),
        P(("tensor", "dp")),
        P("fsdp", ("tensor", "dp")),
        P("fsdp", ("tensor", "dp")),
        P(("tensor", "dp"), "fsdp"),
        P("fsdp", None),
        P("fsdp", None),
    )
    out_specs = P("fsdp", ("tensor", "dp"))
    return jax.shard_map(
        make_body(mesh), mesh=mesh, in_specs=in_specs, out_specs=out_specs, check_vma=False
    )
```

```python
import jax
import jax.numpy as jnp
from jax import lax
from jax.sharding import PartitionSpec as P


norm_eps = 1e-05


def make_body(mesh):
    count_f = mesh.shape["fsdp"]
    count_t = mesh.shape["tensor"]
    count_c = mesh.shape["dp"]
    ring = min(4, max(1, count_f // 2))
    span = count_f // ring
    unit = count_f // (count_t * count_c)

    def send_f(value, step_a, step_b):
        pairs = []
        for a in range(ring):
            for b in range(span):
                pairs.append((a * span + b, ((a + step_a) % ring) * span + (b + step_b) % span))
        return lax.ppermute(value, "fsdp", pairs)

    def send_axis(value, axis, count, step):
        return lax.ppermute(value, axis, [(i, (i + step) % count) for i in range(count)])

    def place(owner):
        t, c = lax.axis_index("tensor"), lax.axis_index("dp")
        block = owner // unit
        block_t, block_c = block // count_c, block % count_c
        near = ((block_c - c) % count_c) * count_t + (block_t - t) % count_t
        return near * unit + owner % unit

    def move_weight(weight, split_axis):
        f = lax.axis_index("fsdp")
        a, b = f // span, f % span
        join_axis = 1 - split_axis
        part = weight.shape[split_axis] // ring
        width = weight.shape[join_axis]
        pieces = [(lax.dynamic_slice_in_dim(weight, a * part, part, split_axis), f)]
        for step in range(1, ring):
            target = (a + step) % ring
            piece = lax.dynamic_slice_in_dim(weight, target * part, part, split_axis)
            pieces.append((send_f(piece, step, 0), ((a - step) % ring) * span + b))
        for piece, owner in list(pieces):
            for step in range(1, span):
                other = (owner // span) * span + (b - step) % span
                pieces.append((send_f(piece, 0, step), other))
        shape = [part, part]
        shape[join_axis] = width * count_f
        whole = jnp.zeros(shape, weight.dtype)
        for piece, owner in pieces:
            whole = lax.dynamic_update_slice_in_dim(whole, piece, place(owner) * width, join_axis)
        return whole

    def block_update(source, norm_gain, gate_weight, up_weight, down_weight):
        capacity, width = source.shape
        features = width * count_t * count_c
        widened = source.astype(jnp.float32)
        mean_square = (
            lax.psum(jnp.sum(widened * widened, axis=-1, keepdims=True), ("tensor", "dp")) / features
        )
        normed = (
            widened * lax.rsqrt(mean_square + norm_eps) * norm_gain.astype(jnp.float32)
        ).astype(jnp.bfloat16)
        gate_full = move_weight(gate_weight, 1)
        up_full = move_weight(up_weight, 1)
        down_full = move_weight(down_weight, 0)
        slots = [normed] + [send_f(normed, k, 0) for k in range(1, ring)]
        columns = [jnp.concatenate(slots, axis=0)]
        for step in range(1, count_t):
            moved = [send_axis(piece, "tensor", count_t, -step) for piece in slots]
            columns.append(jnp.concatenate(moved, axis=0))
        for step in range(1, count_c):
            columns = columns + [send_axis(piece, "dp", count_c, -step) for piece in columns[:count_t]]
        full = jnp.concatenate(columns, axis=1)
        gate_sum = jnp.dot(full, gate_full, preferred_element_type=jnp.float32)
        up_sum = jnp.dot(full, up_full, preferred_element_type=jnp.float32)
        hidden = (jax.nn.silu(gate_sum) * up_sum).astype(jnp.bfloat16)
        half = count_t * width
        total = None
        for slot in list(range(1, ring)) + [0]:
            part = lax.slice_in_dim(hidden, slot * capacity, (slot + 1) * capacity, axis=0)
            products = [
                jnp.dot(
                    part, down_full[:, k * half : (k + 1) * half], preferred_element_type=jnp.float32
                ).astype(jnp.bfloat16)
                for k in range(count_c)
            ]
            own = products[0].astype(jnp.float32)
            for step in range(1, count_c):
                own = own + send_axis(products[step], "dp", count_c, step).astype(jnp.float32)
            own = own.astype(jnp.bfloat16)
            mine = own[:, :width].astype(jnp.float32)
            for step in range(1, count_t):
                away = own[:, step * width : (step + 1) * width]
                moved = send_axis(away, "tensor", count_t, step)
                mine = mine + moved.astype(jnp.float32)
            if slot:
                mine = send_f(mine.astype(jnp.bfloat16), -slot, 0).astype(jnp.float32)
            total = mine if total is None else total + mine
        return total

    def body(states, fresh_rows, norm_gain, gate_weight, up_weight, down_weight, halted, refill_index):
        row_count = states.shape[0]
        running = halted.reshape(row_count) == 0
        capacity = row_count * 3 // 4
        slot_of = jnp.cumsum(running.astype(jnp.int32)) - 1
        slot_ids = lax.iota(jnp.int32, capacity)
        picker = ((slot_of[None, :] == slot_ids[:, None]) & running[None, :]).astype(jnp.bfloat16)
        source = jnp.dot(picker, states, preferred_element_type=jnp.float32).astype(jnp.bfloat16)
        compact = block_update(source, norm_gain, gate_weight, up_weight, down_weight)
        update = jnp.take(compact, jnp.clip(slot_of, 0, capacity - 1), axis=0)
        block_total = refill_index.shape[0]
        batch_len = refill_index.shape[1]
        fresh_blocks = fresh_rows.reshape(block_total, batch_len, fresh_rows.shape[1])
        refilled = jax.vmap(lambda block_rows, pick_index: block_rows[pick_index])(
            fresh_blocks, refill_index
        )
        refilled = refilled.reshape(row_count, fresh_rows.shape[1])
        computed = (states.astype(jnp.float32) + update).astype(jnp.bfloat16)
        return jnp.where(running[:, None], computed, refilled)

    return body


def solution(mesh):
    in_specs = (
        P("fsdp", ("tensor", "dp")),
        P("fsdp", ("tensor", "dp")),
        P(("tensor", "dp")),
        P("fsdp", ("tensor", "dp")),
        P("fsdp", ("tensor", "dp")),
        P(("tensor", "dp"), "fsdp"),
        P("fsdp", None),
        P("fsdp", None),
    )
    out_specs = P("fsdp", ("tensor", "dp"))
    body = make_body(mesh)

    return jax.shard_map(body, mesh=mesh, in_specs=in_specs, out_specs=out_specs, check_vma=False)
```

```python
import jax
import jax.numpy as jnp
from jax import lax
from jax.sharding import PartitionSpec as P


norm_eps = 1e-05


def make_body(mesh):
    count_f = mesh.shape["fsdp"]
    count_t = mesh.shape["tensor"]
    count_c = mesh.shape["dp"]
    ring = min(4, max(1, count_f // 2))
    span = count_f // ring
    unit = count_f // (count_t * count_c)

    def send_f(value, step_a, step_b):
        pairs = []
        for a in range(ring):
            for b in range(span):
                pairs.append((a * span + b, ((a + step_a) % ring) * span + (b + step_b) % span))
        return lax.ppermute(value, "fsdp", pairs)

    def send_axis(value, axis, count, step):
        return lax.ppermute(value, axis, [(i, (i + step) % count) for i in range(count)])

    def place(owner):
        t, c = lax.axis_index("tensor"), lax.axis_index("dp")
        block = owner // unit
        block_t, block_c = block // count_c, block % count_c
        near = ((block_c - c) % count_c) * count_t + (block_t - t) % count_t
        return near * unit + owner % unit

    def move_weight(weight, split_axis):
        f = lax.axis_index("fsdp")
        a, b = f // span, f % span
        join_axis = 1 - split_axis
        part = weight.shape[split_axis] // ring
        width = weight.shape[join_axis]
        pieces = [(lax.dynamic_slice_in_dim(weight, a * part, part, split_axis), f)]
        for step in range(1, ring):
            target = (a + step) % ring
            piece = lax.dynamic_slice_in_dim(weight, target * part, part, split_axis)
            pieces.append((send_f(piece, step, 0), ((a - step) % ring) * span + b))
        for piece, owner in list(pieces):
            for step in range(1, span):
                other = (owner // span) * span + (b - step) % span
                pieces.append((send_f(piece, 0, step), other))
        shape = [part, part]
        shape[join_axis] = width * count_f
        whole = jnp.zeros(shape, weight.dtype)
        for piece, owner in pieces:
            whole = lax.dynamic_update_slice_in_dim(whole, piece, place(owner) * width, join_axis)
        return whole

    def block_update(source, norm_gain, gate_weight, up_weight, down_weight):
        capacity, width = source.shape
        features = width * count_t * count_c
        widened = source.astype(jnp.float32)
        mean_square = (
            lax.psum(jnp.sum(widened * widened, axis=-1, keepdims=True), ("tensor", "dp")) / features
        )
        normed = (
            widened * lax.rsqrt(mean_square + norm_eps) * norm_gain.astype(jnp.float32)
        ).astype(jnp.bfloat16)
        gate_full = move_weight(gate_weight, 1)
        up_full = move_weight(up_weight, 1)
        down_full = move_weight(down_weight, 0)
        slots = [normed] + [send_f(normed, k, 0) for k in range(1, ring)]
        columns = [jnp.concatenate(slots, axis=0)]
        for step in range(1, count_t):
            moved = [send_axis(piece, "tensor", count_t, -step) for piece in slots]
            columns.append(jnp.concatenate(moved, axis=0))
        for step in range(1, count_c):
            columns = columns + [send_axis(piece, "dp", count_c, -step) for piece in columns[:count_t]]
        gate_sum, up_sum = (
            sum(
                jnp.dot(
                    piece,
                    weight[k * width : (k + 1) * width],
                    preferred_element_type=jnp.float32,
                )
                for k, piece in enumerate(columns)
            )
            for weight in (gate_full, up_full)
        )
        hidden = (jax.nn.silu(gate_sum) * up_sum).astype(jnp.bfloat16)
        half = count_t * width
        total = None
        for slot in list(range(1, ring)) + [0]:
            part = lax.slice_in_dim(hidden, slot * capacity, (slot + 1) * capacity, axis=0)
            products = [
                jnp.dot(
                    part, down_full[:, k * half : (k + 1) * half], preferred_element_type=jnp.float32
                ).astype(jnp.bfloat16)
                for k in range(count_c)
            ]
            own = products[0].astype(jnp.float32)
            for step in range(1, count_c):
                own = own + send_axis(products[step], "dp", count_c, step).astype(jnp.float32)
            own = own.astype(jnp.bfloat16)
            mine = own[:, :width].astype(jnp.float32)
            for step in range(1, count_t):
                away = own[:, step * width : (step + 1) * width]
                moved = send_axis(away, "tensor", count_t, step)
                mine = mine + moved.astype(jnp.float32)
            if slot:
                mine = send_f(mine.astype(jnp.bfloat16), -slot, 0).astype(jnp.float32)
            total = mine if total is None else total + mine
        return total

    def body(states, fresh_rows, norm_gain, gate_weight, up_weight, down_weight, halted, refill_index):
        row_count = states.shape[0]
        running = halted.reshape(row_count) == 0
        capacity = row_count * 3 // 4
        slot_of = jnp.cumsum(running.astype(jnp.int32)) - 1
        slot_ids = lax.iota(jnp.int32, capacity)
        picker = ((slot_of[None, :] == slot_ids[:, None]) & running[None, :]).astype(jnp.bfloat16)
        source = jnp.dot(picker, states, preferred_element_type=jnp.float32).astype(jnp.bfloat16)
        compact = block_update(source, norm_gain, gate_weight, up_weight, down_weight)
        update = jnp.take(compact, jnp.clip(slot_of, 0, capacity - 1), axis=0)
        block_total = refill_index.shape[0]
        batch_len = refill_index.shape[1]
        fresh_blocks = fresh_rows.reshape(block_total, batch_len, fresh_rows.shape[1])
        refilled = jax.vmap(lambda block_rows, pick_index: block_rows[pick_index])(
            fresh_blocks, refill_index
        )
        refilled = refilled.reshape(row_count, fresh_rows.shape[1])
        computed = (states.astype(jnp.float32) + update).astype(jnp.bfloat16)
        return jnp.where(running[:, None], computed, refilled)

    return body


def solution(mesh):
    in_specs = (
        P("fsdp", ("tensor", "dp")),
        P("fsdp", ("tensor", "dp")),
        P(("tensor", "dp")),
        P("fsdp", ("tensor", "dp")),
        P("fsdp", ("tensor", "dp")),
        P(("tensor", "dp"), "fsdp"),
        P("fsdp", None),
        P("fsdp", None),
    )
    out_specs = P("fsdp", ("tensor", "dp"))
    body = make_body(mesh)

    return jax.shard_map(body, mesh=mesh, in_specs=in_specs, out_specs=out_specs, check_vma=False)
```

```python
import jax
import jax.numpy as jnp
from jax import lax
from jax.sharding import PartitionSpec as P


norm_eps = 1e-05


def make_body(mesh):
    count_f = mesh.shape["fsdp"]
    count_t = mesh.shape["tensor"]
    count_c = mesh.shape["dp"]
    ring = min(4, max(1, count_f // 2))
    span = count_f // ring
    unit = count_f // (count_t * count_c)

    def send_f(value, step_a, step_b):
        pairs = []
        for a in range(ring):
            for b in range(span):
                pairs.append((a * span + b, ((a + step_a) % ring) * span + (b + step_b) % span))
        return lax.ppermute(value, "fsdp", pairs)

    def send_line(value, senders, step):
        pairs = [(a * span + b, (a + step) * span + b) for a in senders for b in range(span)]
        return lax.ppermute(value, "fsdp", pairs)

    def send_axis(value, axis, count, step):
        return lax.ppermute(value, axis, [(i, (i + step) % count) for i in range(count)])

    def place(owner):
        t, c = lax.axis_index("tensor"), lax.axis_index("dp")
        block = owner // unit
        block_t, block_c = block // count_c, block % count_c
        near = ((block_c - c) % count_c) * count_t + (block_t - t) % count_t
        return near * unit + owner % unit

    def move_weight(weight, split_axis):
        f = lax.axis_index("fsdp")
        a, b = f // span, f % span
        join_axis = 1 - split_axis
        part = weight.shape[split_axis] // ring
        width = weight.shape[join_axis]
        pieces = [(lax.dynamic_slice_in_dim(weight, a * part, part, split_axis), f)]
        for step in range(1, ring):
            target = (a + step) % ring
            piece = lax.dynamic_slice_in_dim(weight, target * part, part, split_axis)
            pieces.append((send_f(piece, step, 0), ((a - step) % ring) * span + b))
        for piece, owner in list(pieces):
            for step in range(1, span):
                other = (owner // span) * span + (b - step) % span
                pieces.append((send_f(piece, 0, step), other))
        shape = [part, part]
        shape[join_axis] = width * count_f
        whole = jnp.zeros(shape, weight.dtype)
        for piece, owner in pieces:
            whole = lax.dynamic_update_slice_in_dim(whole, piece, place(owner) * width, join_axis)
        return whole

    def block_update(source, norm_gain, gate_weight, up_weight, down_weight):
        capacity, width = source.shape
        features = width * count_t * count_c
        widened = source.astype(jnp.float32)
        mean_square = (
            lax.psum(jnp.sum(widened * widened, axis=-1, keepdims=True), ("tensor", "dp")) / features
        )
        normed = (
            widened * lax.rsqrt(mean_square + norm_eps) * norm_gain.astype(jnp.float32)
        ).astype(jnp.bfloat16)
        gate_full = move_weight(gate_weight, 1)
        up_full = move_weight(up_weight, 1)
        down_full = move_weight(down_weight, 0)
        a = lax.axis_index("fsdp") // span
        rightward, leftward = [normed], [normed]
        for k in range(1, ring):
            rightward.append(send_line(rightward[-1], range(k - 1, ring - 1), 1))
            leftward.append(send_line(leftward[-1], range(1, ring - k + 1), -1))
        slots = [normed] + [
            jnp.where(a >= k, rightward[k], leftward[ring - k]) for k in range(1, ring)
        ]
        columns = [jnp.concatenate(slots, axis=0)]
        for step in range(1, count_t):
            moved = [send_axis(piece, "tensor", count_t, -step) for piece in slots]
            columns.append(jnp.concatenate(moved, axis=0))
        for step in range(1, count_c):
            columns = columns + [send_axis(piece, "dp", count_c, -step) for piece in columns[:count_t]]
        gate_sum, up_sum = (
            sum(
                jnp.dot(
                    piece,
                    weight[k * width : (k + 1) * width],
                    preferred_element_type=jnp.float32,
                )
                for k, piece in enumerate(columns)
            )
            for weight in (gate_full, up_full)
        )
        hidden = (jax.nn.silu(gate_sum) * up_sum).astype(jnp.bfloat16)
        half = count_t * width
        sums = {}
        for slot in sorted(range(1, ring), key=lambda k: -abs(2 * k - ring)) + [0]:
            part = lax.slice_in_dim(hidden, slot * capacity, (slot + 1) * capacity, axis=0)
            products = [
                jnp.dot(
                    part, down_full[:, k * half : (k + 1) * half], preferred_element_type=jnp.float32
                ).astype(jnp.bfloat16)
                for k in range(count_c)
            ]
            own = products[0].astype(jnp.float32)
            for step in range(1, count_c):
                own = own + send_axis(products[step], "dp", count_c, step).astype(jnp.float32)
            own = own.astype(jnp.bfloat16)
            mine = own[:, :width].astype(jnp.float32)
            for step in range(1, count_t):
                away = own[:, step * width : (step + 1) * width]
                moved = send_axis(away, "tensor", count_t, step)
                mine = mine + moved.astype(jnp.float32)
            sums[slot] = mine
        total = sums[0]
        right = left = None
        for k in range(ring - 1, 0, -1):
            own_right, own_left = sums[ring - k], sums[k]
            if right is not None:
                own_right, own_left = own_right + right, own_left + left
            right = send_line(own_right.astype(jnp.bfloat16), range(ring - k), 1)
            left = send_line(own_left.astype(jnp.bfloat16), range(k, ring), -1)
            right, left = right.astype(jnp.float32), left.astype(jnp.float32)
        if right is not None:
            total = total + right + left
        return total

    def body(states, fresh_rows, norm_gain, gate_weight, up_weight, down_weight, halted, refill_index):
        row_count = states.shape[0]
        running = halted.reshape(row_count) == 0
        capacity = row_count * 3 // 4
        slot_of = jnp.cumsum(running.astype(jnp.int32)) - 1
        slot_ids = lax.iota(jnp.int32, capacity)
        picker = ((slot_of[None, :] == slot_ids[:, None]) & running[None, :]).astype(jnp.bfloat16)
        source = jnp.dot(picker, states, preferred_element_type=jnp.float32).astype(jnp.bfloat16)
        compact = block_update(source, norm_gain, gate_weight, up_weight, down_weight)
        update = jnp.take(compact, jnp.clip(slot_of, 0, capacity - 1), axis=0)
        block_total = refill_index.shape[0]
        batch_len = refill_index.shape[1]
        fresh_blocks = fresh_rows.reshape(block_total, batch_len, fresh_rows.shape[1])
        refilled = jax.vmap(lambda block_rows, pick_index: block_rows[pick_index])(
            fresh_blocks, refill_index
        )
        refilled = refilled.reshape(row_count, fresh_rows.shape[1])
        computed = (states.astype(jnp.float32) + update).astype(jnp.bfloat16)
        return jnp.where(running[:, None], computed, refilled)

    return body


def solution(mesh):
    in_specs = (
        P("fsdp", ("tensor", "dp")),
        P("fsdp", ("tensor", "dp")),
        P(("tensor", "dp")),
        P("fsdp", ("tensor", "dp")),
        P("fsdp", ("tensor", "dp")),
        P(("tensor", "dp"), "fsdp"),
        P("fsdp", None),
        P("fsdp", None),
    )
    out_specs = P("fsdp", ("tensor", "dp"))
    body = make_body(mesh)

    return jax.shard_map(body, mesh=mesh, in_specs=in_specs, out_specs=out_specs, check_vma=False)
```

```python
import jax
import jax.numpy as jnp
from jax import lax
from jax.sharding import PartitionSpec as P


norm_eps = 1e-05


def make_body(mesh):
    count_f = mesh.shape["fsdp"]
    count_t = mesh.shape["tensor"]
    count_c = mesh.shape["dp"]
    ring = min(4, max(1, count_f // 2))
    span = count_f // ring
    unit = count_f // (count_t * count_c)

    def send_f(value, step_a, step_b):
        pairs = []
        for a in range(ring):
            for b in range(span):
                pairs.append((a * span + b, ((a + step_a) % ring) * span + (b + step_b) % span))
        return lax.ppermute(value, "fsdp", pairs)

    def send_line(value, senders, step):
        pairs = [(a * span + b, (a + step) * span + b) for a in senders for b in range(span)]
        return lax.ppermute(value, "fsdp", pairs)

    def send_axis(value, axis, count, step):
        return lax.ppermute(value, axis, [(i, (i + step) % count) for i in range(count)])

    def place(owner):
        t, c = lax.axis_index("tensor"), lax.axis_index("dp")
        block = owner // unit
        block_t, block_c = block // count_c, block % count_c
        near = ((block_c - c) % count_c) * count_t + (block_t - t) % count_t
        return near * unit + owner % unit

    def move_weight(weight, split_axis):
        f = lax.axis_index("fsdp")
        a, b = f // span, f % span
        join_axis = 1 - split_axis
        part = weight.shape[split_axis] // ring
        width = weight.shape[join_axis]
        pieces = [(lax.dynamic_slice_in_dim(weight, a * part, part, split_axis), f)]
        for step in range(1, ring):
            target = (a + step) % ring
            piece = lax.dynamic_slice_in_dim(weight, target * part, part, split_axis)
            pieces.append((send_f(piece, step, 0), ((a - step) % ring) * span + b))
        for piece, owner in list(pieces):
            for step in range(1, span):
                other = (owner // span) * span + (b - step) % span
                pieces.append((send_f(piece, 0, step), other))
        shape = [part, part]
        shape[join_axis] = width * count_f
        whole = jnp.zeros(shape, weight.dtype)
        for piece, owner in pieces:
            whole = lax.dynamic_update_slice_in_dim(whole, piece, place(owner) * width, join_axis)
        return whole

    def block_update(source, norm_gain, gate_weight, up_weight, down_weight):
        capacity, width = source.shape
        features = width * count_t * count_c
        widened = source.astype(jnp.float32)
        mean_square = (
            lax.psum(jnp.sum(widened * widened, axis=-1, keepdims=True), ("tensor", "dp")) / features
        )
        normed = (
            widened * lax.rsqrt(mean_square + norm_eps) * norm_gain.astype(jnp.float32)
        ).astype(jnp.bfloat16)
        gate_full = move_weight(gate_weight, 1)
        up_full = move_weight(up_weight, 1)
        down_full = move_weight(down_weight, 0)
        a = lax.axis_index("fsdp") // span
        rightward, leftward = [normed], [normed]
        for k in range(1, ring):
            rightward.append(send_line(rightward[-1], range(k - 1, ring - 1), 1))
            leftward.append(send_line(leftward[-1], range(1, ring - k + 1), -1))
        slots = [normed] + [
            jnp.where(a >= k, rightward[k], leftward[ring - k]) for k in range(1, ring)
        ]
        columns = [jnp.concatenate(slots, axis=0)]
        for step in range(1, count_t):
            moved = [send_axis(piece, "tensor", count_t, -step) for piece in slots]
            columns.append(jnp.concatenate(moved, axis=0))
        for step in range(1, count_c):
            columns = columns + [send_axis(piece, "dp", count_c, -step) for piece in columns[:count_t]]
        gate_sum, up_sum = (
            sum(
                jnp.dot(
                    piece,
                    weight[k * width : (k + 1) * width],
                    preferred_element_type=jnp.float32,
                )
                for k, piece in enumerate(columns)
            )
            for weight in (gate_full, up_full)
        )
        hidden = (jax.nn.silu(gate_sum) * up_sum).astype(jnp.bfloat16)
        half = count_t * width
        total = None
        for slot in list(range(1, ring)) + [0]:
            part = lax.slice_in_dim(hidden, slot * capacity, (slot + 1) * capacity, axis=0)
            products = [
                jnp.dot(
                    part, down_full[:, k * half : (k + 1) * half], preferred_element_type=jnp.float32
                ).astype(jnp.bfloat16)
                for k in range(count_c)
            ]
            own = products[0].astype(jnp.float32)
            for step in range(1, count_c):
                own = own + send_axis(products[step], "dp", count_c, step).astype(jnp.float32)
            own = own.astype(jnp.bfloat16)
            mine = own[:, :width].astype(jnp.float32)
            for step in range(1, count_t):
                away = own[:, step * width : (step + 1) * width]
                moved = send_axis(away, "tensor", count_t, step)
                mine = mine + moved.astype(jnp.float32)
            if slot:
                mine = send_f(mine.astype(jnp.bfloat16), -slot, 0).astype(jnp.float32)
            total = mine if total is None else total + mine
        return total

    def body(states, fresh_rows, norm_gain, gate_weight, up_weight, down_weight, halted, refill_index):
        row_count = states.shape[0]
        running = halted.reshape(row_count) == 0
        capacity = row_count * 3 // 4
        slot_of = jnp.cumsum(running.astype(jnp.int32)) - 1
        slot_ids = lax.iota(jnp.int32, capacity)
        picker = ((slot_of[None, :] == slot_ids[:, None]) & running[None, :]).astype(jnp.bfloat16)
        source = jnp.dot(picker, states, preferred_element_type=jnp.float32).astype(jnp.bfloat16)
        compact = block_update(source, norm_gain, gate_weight, up_weight, down_weight)
        update = jnp.take(compact, jnp.clip(slot_of, 0, capacity - 1), axis=0)
        block_total = refill_index.shape[0]
        batch_len = refill_index.shape[1]
        fresh_blocks = fresh_rows.reshape(block_total, batch_len, fresh_rows.shape[1])
        refilled = jax.vmap(lambda block_rows, pick_index: block_rows[pick_index])(
            fresh_blocks, refill_index
        )
        refilled = refilled.reshape(row_count, fresh_rows.shape[1])
        computed = (states.astype(jnp.float32) + update).astype(jnp.bfloat16)
        return jnp.where(running[:, None], computed, refilled)

    return body


def solution(mesh):
    in_specs = (
        P("fsdp", ("tensor", "dp")),
        P("fsdp", ("tensor", "dp")),
        P(("tensor", "dp")),
        P("fsdp", ("tensor", "dp")),
        P("fsdp", ("tensor", "dp")),
        P(("tensor", "dp"), "fsdp"),
        P("fsdp", None),
        P("fsdp", None),
    )
    out_specs = P("fsdp", ("tensor", "dp"))
    body = make_body(mesh)

    return jax.shard_map(body, mesh=mesh, in_specs=in_specs, out_specs=out_specs, check_vma=False)
```
